32 devices in a mesh: mem: 8 (over z, x), head: 4 (over y, core).
Axes of the slice: x: 2, y: 2, z: 4, core: 2. Of those that a mesh axis runs over, the one named last changes fastest.
Arguments:
- tokens: bfloat16 [8192, 4096], P('mem'), may hold values from -14 to 14
- w_query: bfloat16 [4096, 4096], P(None, 'head'), may hold values from -0.09375 to 0.09375
- w_key: bfloat16 [4096, 1024], P(None, 'head'), may hold values from -0.09375 to 0.09375
- w_value: bfloat16 [4096, 1024], P(None, 'head'), may hold values from -0.09375 to 0.09375
- w_out: bfloat16 [4096, 4096], P('head'), may hold values from -0.09375 to 0.09375
- gate_bias: float32 [32], P('head'), may hold values from -4 to 4
- mem_keys: bfloat16 [65536, 1024], P('mem', 'head'), may hold values from -72 to 72
- mem_values: bfloat16 [65536, 1024], P('mem', 'head'), may hold values from -6 to 6
- block_ids: int32 [64, 16], P('mem'), may hold values from 0 to 511, as said below
- block_counts: int32 [512], replicated, may hold values from 1 to 128
Outputs:
- layer_out: bfloat16 [8192, 4096], P('mem', 'head')
The draws below stay inside these ranges and needn't reach their ends.
Inputs may be any that keep to these rules, and one draw needn't show every extreme that they name: `block_ids`: row c lists 16 different memory blocks; block b lies on index b // 64 of mem. Over the 8 query blocks of one index of mem, every listed block appears in exactly two rows, at most 16 different listed blocks lie on any one index of mem, and in every draw some index of mem has exactly 16 different blocks listed by every index of mem.
All inputs are finite; a program needn't handle non-finite values.
Results may differ from the reference program's by a relative error of at most 0.015.
The reference program's roundings to bfloat16 on the way count: a program that leaves them out, or rounds other values in their place, can miss the bound.
Values may be sent and summed in bfloat16 or wider, within the bound.
A program may use at most 320 MiB of HBM per device.

```python
import jax
import jax.numpy as jnp
from jax import lax

D = 4096
HEADS = 32
KV_HEADS = 8
HD = 128
BLK = 128
TOPK = 16
TOK_DEV = 1024
MB_DEV = 64
TOKENS = 8192
QB_DEV = 8
QBLOCKS = 64
MEM_BLOCKS = 512
MEM_TOKENS = 65536
DCAP = 16
N_MEM = 8
N_HEAD = 4


def draw_tokens(key, part):
    first_key = jax.random.fold_in(jax.random.fold_in(key, 11), 0)
    return jnp.clip(jax.random.normal(first_key, (TOKENS, D), jnp.float32), -6.0, 6.0).astype(jnp.bfloat16)


def draw_mem_keys(key, part):
    first_key = jax.random.fold_in(jax.random.fold_in(key, 23), 0)
    row_count = MEM_TOKENS
    col_count = KV_HEADS * HD
    return jnp.clip(jax.random.normal(first_key, (row_count, col_count), jnp.float32), -6.0, 6.0).astype(jnp.bfloat16)


def draw_block_ids(key, part):
    owners_n = MEM_BLOCKS // MB_DEV
    unique_n = QB_DEV * TOPK // 2
    hot_owner = jax.random.randint(jax.random.fold_in(key, 1), (), 0, owners_n).astype(jnp.int32)

    def one_segment(seg_key):
        key_one, key_two, key_three = jax.random.split(seg_key, 3)
        others = (hot_owner + 1 + jnp.arange((owners_n - 1) * DCAP, dtype=jnp.int32) // DCAP) % owners_n
        others = jax.random.permutation(key_one, others)
        hot_part = jnp.zeros((DCAP,), jnp.int32) + hot_owner
        pool = jnp.concatenate([hot_part, others.astype(jnp.int32)])[:unique_n]
        pool = jax.random.permutation(key_two, pool)
        order = jnp.arange(unique_n)
        earlier_same = (pool[:, None] == pool[None, :]) & (order[None, :] < order[:, None])
        occurrence = jnp.sum(earlier_same.astype(jnp.int32), axis=1)
        local_table = jnp.tile(jnp.arange(MB_DEV, dtype=jnp.int32)[None, :], (owners_n, 1))
        local_table = jax.random.permutation(key_three, local_table, axis=1, independent=True)
        chosen = pool * MB_DEV + local_table[pool, occurrence]
        row_pick = (jnp.arange(QB_DEV)[:, None] * (TOPK // 2) + jnp.arange(TOPK)[None, :]) % unique_n
        return chosen[row_pick]
    seg_keys = jax.random.split(jax.random.fold_in(key, 2), owners_n)
    return jax.vmap(one_segment)(seg_keys).reshape(owners_n * QB_DEV, TOPK).astype(jnp.int32)


def plant(values, key, low, top_value):
    longest = values.shape.index(max(values.shape))
    spots = []
    for shift in (0, 1):
        where = [jax.random.randint(jax.random.fold_in(key, axis), (), 0, length) for axis, length in enumerate(values.shape)]
        where[longest] = (where[longest] + shift) % values.shape[longest]
        spots.append(tuple(where))
    return values.at[spots[0]].set(low).at[spots[1]].set(top_value)


def shard_levels(own_key, dims, cuts, least, high):
    level, own = 1.0, jax.random.fold_in(own_key, 6)
    for axis_at, blocks in cuts:
        heights = jnp.exp(jax.random.uniform(jax.random.fold_in(own, axis_at), (blocks,), jnp.float32, least / len(cuts), high / len(cuts)))
        level = level * jnp.repeat(heights, dims[axis_at] // blocks).reshape([-1 if axis == axis_at else 1 for axis in range(len(dims))])
    return level


def centred(key, shape, width, bound, shards=(), kind=jnp.bfloat16):
    drawn = width * jax.random.normal(key, shape, jnp.float32)
    if shards:
        drawn = drawn * shard_levels(key, shape, shards, -0.22, 0.18)
    return jnp.clip(drawn, -bound, bound).astype(kind)


def setup_inputs(seed: int = 0) -> dict:
    seeds = jax.random.split(jax.random.key(seed), 11)
    return {
        "tokens": draw_tokens(jax.random.fold_in(seeds[10], 71), 0),
        "w_query": centred(seeds[1], (D, HEADS * HD), D ** -0.5, 0.09375, ((1, 4),)),
        "w_key": centred(seeds[2], (D, KV_HEADS * HD), D ** -0.5, 0.09375, ((1, 4),)),
        "w_value": centred(seeds[3], (D, KV_HEADS * HD), D ** -0.5, 0.09375, ((1, 4),)),
        "w_out": centred(seeds[4], (HEADS * HD, D), (HEADS * HD) ** -0.5, 0.09375, ((0, 4),)),
        "gate_bias": centred(seeds[5], (HEADS,), 1.5, 4.0, ((0, 4),), jnp.float32),
        "mem_keys": draw_mem_keys(jax.random.fold_in(seeds[10], 71), 0),
        "mem_values": centred(seeds[7], (MEM_TOKENS, KV_HEADS * HD), 1.0, 6.0, ((0, 8), (1, 4))),
        "block_ids": draw_block_ids(jax.random.fold_in(seeds[10], 71), 0),
        "block_counts": plant(jax.random.randint(seeds[9], (MEM_BLOCKS,), 1, BLK + 1), jax.random.fold_in(seeds[9], 1), 1, BLK).astype(jnp.int32),
    }


def attend(queries, key_rows, value_rows, allowed):
    scores = jnp.einsum("qkgd,skd->kgqs", queries.astype(jnp.float32), key_rows.astype(jnp.float32)) * (HD ** -0.5)
    scores = jnp.where(allowed, scores, -jnp.inf)
    peak_score = jnp.max(scores, axis=-1, keepdims=True)
    weights = jnp.exp(scores - peak_score)
    weights = (weights / jnp.sum(weights, axis=-1, keepdims=True)).astype(jnp.bfloat16)
    return jnp.einsum("kgqs,skd->qkgd", weights.astype(jnp.float32), value_rows.astype(jnp.float32))


def reference(tokens, w_query, w_key, w_value, w_out, gate_bias, mem_keys, mem_values, block_ids, block_counts):
    per_kv = HEADS // KV_HEADS
    queries = jnp.dot(tokens, w_query, preferred_element_type=jnp.float32).astype(jnp.bfloat16)
    local_keys = jnp.dot(tokens, w_key, preferred_element_type=jnp.float32).astype(jnp.bfloat16)
    local_values = jnp.dot(tokens, w_value, preferred_element_type=jnp.float32).astype(jnp.bfloat16)
    causal = jnp.arange(TOK_DEV)[None, :] <= jnp.arange(TOK_DEV)[:, None]

    def local_segment(inputs):
        q_seg, k_seg, v_seg = inputs
        return attend(q_seg, k_seg, v_seg, causal[None, None])

    local_out = lax.map(local_segment, (queries.reshape(N_MEM, TOK_DEV, KV_HEADS, per_kv, HD),
                                        local_keys.reshape(N_MEM, TOK_DEV, KV_HEADS, HD),
                                        local_values.reshape(N_MEM, TOK_DEV, KV_HEADS, HD)))
    local_out = local_out.reshape(TOKENS, KV_HEADS, per_kv, HD)
    key_blocks = mem_keys.reshape(MEM_BLOCKS, BLK, KV_HEADS, HD)
    value_blocks = mem_values.reshape(MEM_BLOCKS, BLK, KV_HEADS, HD)
    position = jnp.arange(BLK)

    def memory_block(inputs):
        q_blk, chosen = inputs
        picked_keys = key_blocks[chosen].reshape(TOPK * BLK, KV_HEADS, HD)
        picked_values = value_blocks[chosen].reshape(TOPK * BLK, KV_HEADS, HD)
        allowed = (position[None, :] < block_counts[chosen][:, None]).reshape(TOPK * BLK)
        return attend(q_blk, picked_keys, picked_values, allowed[None, None, None, :])

    mem_out = lax.map(memory_block, (queries.reshape(QBLOCKS, BLK, KV_HEADS, per_kv, HD), block_ids))
    mem_out = mem_out.reshape(TOKENS, KV_HEADS, per_kv, HD)
    gate = jax.nn.sigmoid(gate_bias.astype(jnp.float32)).reshape(KV_HEADS, per_kv)[None, :, :, None]
    attn = (gate * mem_out + (1.0 - gate) * local_out).astype(jnp.bfloat16).reshape(TOKENS, HEADS * HD)
    slab_width = HEADS * HD // N_HEAD
    running = jnp.zeros((TOKENS, D), jnp.float32)
    for group_index in range(N_HEAD):
        lower = group_index * slab_width
        partial_sum = jnp.dot(attn[:, lower:lower + slab_width], w_out[lower:lower + slab_width],
                              preferred_element_type=jnp.float32).astype(jnp.bfloat16)
        running = running + lax.optimization_barrier(partial_sum).astype(jnp.float32)
    return running.astype(jnp.bfloat16)
```

```python
import functools

import jax
import jax.numpy as jnp
from jax import lax
from jax.experimental import pallas as pl
from jax.experimental.pallas import tpu as pltpu
from jax.sharding import PartitionSpec as P

HD = 128
BLK = 128
LOG2E = 1.4426950408889634
MIB = 1 << 20


def share_ids_kernel(owners, ids_ref, out_ref, send_sem, recv_sem):
    me = lax.axis_index("mem")
    barrier = pltpu.get_barrier_semaphore()
    for step in range(1, owners):
        peer = lax.rem(me + step, owners)
        pl.semaphore_signal(
            barrier, inc=1, device_id={"mem": peer}, device_id_type=pl.DeviceIdType.MESH
        )
    pl.semaphore_wait(barrier, owners - 1)
    copies = []
    for step in range(1, owners):
        peer = lax.rem(me + step, owners)
        copy = pltpu.make_async_remote_copy(
            src_ref=ids_ref,
            dst_ref=out_ref.at[me],
            send_sem=send_sem.at[step],
            recv_sem=recv_sem.at[step],
            device_id={"mem": peer},
            device_id_type=pl.DeviceIdType.MESH,
        )
        copy.start()
        copies.append(copy)
    out_ref[me] = ids_ref[...]
    for copy in copies:
        copy.wait()


def share_ids(ids, owners):
    return pl.pallas_call(
        functools.partial(share_ids_kernel, owners),
        out_shape=jax.ShapeDtypeStruct((owners,) + ids.shape, ids.dtype),
        in_specs=[pl.BlockSpec(memory_space=pltpu.VMEM)],
        out_specs=pl.BlockSpec(memory_space=pltpu.VMEM),
        scratch_shapes=[
            pltpu.SemaphoreType.DMA((owners,)),
            pltpu.SemaphoreType.DMA((owners,)),
        ],
        compiler_params=pltpu.CompilerParams(collective_id=0, has_side_effects=True),
        name="share_ids",
    )(ids)


def softmax_rows(scores):
    peak = jnp.max(scores, axis=-1, keepdims=True)
    weights = jnp.exp2((scores - peak) * (LOG2E * HD ** -0.5))
    total = jnp.sum(weights, axis=-1, keepdims=True)
    return (weights * (1.0 / total)).astype(jnp.bfloat16)


def local_kernel(per_kv, q_ref, k_ref, v_ref, out_ref):
    start = pl.program_id(1) * BLK
    keys = k_ref[...]
    values = v_ref[...]
    shape = (BLK, keys.shape[0])
    seen = lax.broadcasted_iota(jnp.int32, shape, 1) <= (
        lax.broadcasted_iota(jnp.int32, shape, 0) + start
    )
    for head in range(per_kv):
        cols = slice(head * HD, (head + 1) * HD)
        scores = lax.dot_general(
            q_ref[:, cols], keys, (((1,), (1,)), ((), ())), preferred_element_type=jnp.float32
        )
        weights = softmax_rows(jnp.where(seen, scores, -jnp.inf))
        out_ref[:, cols] = jnp.dot(weights, values, preferred_element_type=jnp.float32)


def local_attention(queries, keys, values, kv_local, per_kv):
    rows = queries.shape[0]
    width = per_kv * HD
    return pl.pallas_call(
        functools.partial(local_kernel, per_kv),
        grid=(kv_local, rows // BLK),
        in_specs=[
            pl.BlockSpec((BLK, width), lambda j, c: (c, j)),
            pl.BlockSpec((rows, HD), lambda j, c: (0, j)),
            pl.BlockSpec((rows, HD), lambda j, c: (0, j)),
        ],
        out_specs=pl.BlockSpec((BLK, width), lambda j, c: (c, j)),
        out_shape=jax.ShapeDtypeStruct(queries.shape, jnp.float32),
        compiler_params=pltpu.CompilerParams(vmem_limit_bytes=40 * MIB),
        cost_estimate=pl.CostEstimate(
            flops=4 * rows * rows * queries.shape[1],
            bytes_accessed=6 * rows * queries.shape[1],
            transcendentals=rows * rows * kv_local * per_kv,
        ),
        name="local_attention",
    )(queries, keys, values)


def weights_kernel(per_kv, topk, slot_ref, q_ref, bias_ref, k_ref, out_ref, picked):
    block = pl.program_id(1)
    for pick in range(topk):
        picked[pick * BLK : (pick + 1) * BLK, :] = k_ref[slot_ref[block * topk + pick]]
    keys = picked[...]
    bias = bias_ref[0]
    for head in range(per_kv):
        scores = lax.dot_general(
            q_ref[:, head * HD : (head + 1) * HD],
            keys,
            (((1,), (1,)), ((), ())),
            preferred_element_type=jnp.float32,
        )
        out_ref[0, 0, head] = softmax_rows(scores + bias)


def memory_weights(slots, queries, bias, keys, kv_local, per_kv, topk):
    rows = queries.shape[0]
    blocks = rows // BLK
    width = topk * BLK
    total = keys.shape[0]
    return pl.pallas_call(
        functools.partial(weights_kernel, per_kv, topk),
        grid_spec=pltpu.PrefetchScalarGridSpec(
            num_scalar_prefetch=1,
            grid=(kv_local, blocks),
            in_specs=[
                pl.BlockSpec((BLK, per_kv * HD), lambda j, c, s: (c, j)),
                pl.BlockSpec((1, 1, width), lambda j, c, s: (c, 0, 0)),
                pl.BlockSpec((total, BLK, HD), lambda j, c, s: (0, 0, j)),
            ],
            out_specs=pl.BlockSpec(
                (1, 1, per_kv, BLK, width), lambda j, c, s: (j, c, 0, 0, 0)
            ),
            scratch_shapes=[pltpu.VMEM((width, HD), jnp.bfloat16)],
        ),
        out_shape=jax.ShapeDtypeStruct((kv_local, blocks, per_kv, BLK, width), jnp.bfloat16),
        compiler_params=pltpu.CompilerParams(vmem_limit_bytes=48 * MIB),
        cost_estimate=pl.CostEstimate(
            flops=2 * rows * width * queries.shape[1],
            bytes_accessed=2 * kv_local * per_kv * rows * width,
            transcendentals=rows * width * kv_local * per_kv,
        ),
        name="memory_weights",
    )(slots, queries, bias, keys)


def mix_kernel(per_kv, topk, slot_ref, w_ref, gate_ref, local_ref, v_ref, out_ref, picked):
    block = pl.program_id(1)
    for pick in range(topk):
        picked[pick * BLK : (pick + 1) * BLK, :] = v_ref[slot_ref[block * topk + pick]]
    values = picked[...]
    for head in range(per_kv):
        cols = slice(head * HD, (head + 1) * HD)
        mem_out = jnp.dot(w_ref[0, 0, head], values, preferred_element_type=jnp.float32)
        gate = gate_ref[:, cols]
        out_ref[:, cols] = (gate * mem_out + (1.0 - gate) * local_ref[:, cols]).astype(
            jnp.bfloat16
        )


def mix_values(slots, weights, gate, local_out, values, kv_local, per_kv, topk):
    rows, cols = local_out.shape
    blocks = rows // BLK
    width = topk * BLK
    total = values.shape[0]
    return pl.pallas_call(
        functools.partial(mix_kernel, per_kv, topk),
        grid_spec=pltpu.PrefetchScalarGridSpec(
            num_scalar_prefetch=1,
            grid=(kv_local, blocks),
            in_specs=[
                pl.BlockSpec((1, 1, per_kv, BLK, width), lambda j, c, s: (j, c, 0, 0, 0)),
                pl.BlockSpec((1, per_kv * HD), lambda j, c, s: (0, j)),
                pl.BlockSpec((BLK, per_kv * HD), lambda j, c, s: (c, j)),
                pl.BlockSpec((total, BLK, HD), lambda j, c, s: (0, 0, j)),
            ],
            out_specs=pl.BlockSpec((BLK, per_kv * HD), lambda j, c, s: (c, j)),
            scratch_shapes=[pltpu.VMEM((width, HD), jnp.bfloat16)],
        ),
        out_shape=jax.ShapeDtypeStruct((rows, cols), jnp.bfloat16),
        compiler_params=pltpu.CompilerParams(vmem_limit_bytes=48 * MIB),
        cost_estimate=pl.CostEstimate(
            flops=2 * rows * width * cols,
            bytes_accessed=2 * kv_local * per_kv * rows * width,
            transcendentals=0,
        ),
        name="mix_values",
    )(slots, weights, gate, local_out, values)


def plan_requests(flat_chosen, blocks_each):
    owner_of = flat_chosen // blocks_each
    local_of = flat_chosen % blocks_each
    order = jnp.arange(flat_chosen.shape[0])
    repeated = (flat_chosen[:, None] == flat_chosen[None, :]) & (order[None, :] < order[:, None])
    first_seen = jnp.logical_not(jnp.any(repeated, axis=1))
    below = (owner_of[:, None] == owner_of[None, :]) & (flat_chosen[None, :] < flat_chosen[:, None])
    rank_of = jnp.sum((below & first_seen[None, :]).astype(jnp.int32), axis=1)
    return (owner_of, local_of, rank_of, first_seen)


def on_device(
    tokens, w_query, w_key, w_value, w_out, gate_bias, mem_keys, mem_values, block_ids, block_counts
):
    tok_rows = tokens.shape[0]
    qblk_count = tok_rows // BLK
    topk_count = block_ids.shape[1]
    kv_local = w_key.shape[1] // HD
    heads_local = w_query.shape[1] // HD
    per_kv = heads_local // kv_local
    owners = lax.axis_size("mem")
    blocks_each = mem_keys.shape[0] // BLK
    me_index = lax.axis_index("mem")
    capacity = max(2, topk_count * qblk_count // owners)
    all_chosen = share_ids(block_ids, owners).reshape(owners, qblk_count * topk_count)

    def send_list(flat_chosen):
        owner_of, local_of, rank_of, first_seen = plan_requests(flat_chosen, blocks_each)
        wanted = (owner_of == me_index) & first_seen
        select = wanted[None, :] & (rank_of[None, :] == jnp.arange(capacity)[:, None])
        return jnp.sum(select.astype(jnp.int32) * local_of[None, :], axis=1)

    send_slots = jax.vmap(send_list)(all_chosen)
    key_blocks = mem_keys.reshape(blocks_each, BLK, kv_local * HD)
    value_blocks = mem_values.reshape(blocks_each, BLK, kv_local * HD)
    got_keys = lax.all_to_all(
        key_blocks[send_slots], "mem", split_axis=0, concat_axis=0, tiled=True
    ).reshape(owners * capacity, BLK, kv_local * HD)
    got_values = lax.all_to_all(
        value_blocks[send_slots], "mem", split_axis=0, concat_axis=0, tiled=True
    ).reshape(owners * capacity, BLK, kv_local * HD)
    queries = jnp.dot(tokens, w_query, preferred_element_type=jnp.float32).astype(jnp.bfloat16)
    local_keys = jnp.dot(tokens, w_key, preferred_element_type=jnp.float32).astype(jnp.bfloat16)
    local_values = jnp.dot(tokens, w_value, preferred_element_type=jnp.float32).astype(jnp.bfloat16)
    local_out = local_attention(queries, local_keys, local_values, kv_local, per_kv)
    own_flat = block_ids.reshape(-1)
    owner_of, local_of, rank_of, first_seen = plan_requests(own_flat, blocks_each)
    slot_of = owner_of * capacity + rank_of
    total_blocks = block_counts.shape[0]
    filled = jnp.sum(
        jnp.where(own_flat[:, None] == jnp.arange(total_blocks)[None, :], block_counts[None, :], 0),
        axis=1,
    )
    bias = jnp.where(jnp.arange(BLK)[None, :] < filled[:, None], 0.0, -jnp.inf)
    bias = bias.reshape(qblk_count, 1, topk_count * BLK).astype(jnp.float32)
    weights = memory_weights(slot_of, queries, bias, got_keys, kv_local, per_kv, topk_count)
    gate = jnp.repeat(jax.nn.sigmoid(gate_bias), HD).reshape(1, heads_local * HD)
    attn = mix_values(
        slot_of, weights, gate, local_out, got_values, kv_local, per_kv, topk_count
    )
    terms = jnp.dot(attn, w_out, preferred_element_type=jnp.float32)
    return lax.psum_scatter(terms.astype(jnp.bfloat16), "head", scatter_dimension=1, tiled=True)


def solution(mesh):
    in_specs = (
        P("mem", None),
        P(None, "head"),
        P(None, "head"),
        P(None, "head"),
        P("head", None),
        P("head"),
        P("mem", "head"),
        P("mem", "head"),
        P("mem", None),
        P(),
    )
    out_specs = P("mem", "head")
    return jax.shard_map(
        on_device, mesh=mesh, in_specs=in_specs, out_specs=out_specs, check_vma=False
    )
```

```python
import functools

import jax
import jax.numpy as jnp
from jax import lax
from jax.experimental import pallas as pl
from jax.experimental.pallas import tpu as pltpu
from jax.sharding import PartitionSpec as P

HD = 128
BLK = 128
LOG2E = 1.4426950408889634
MIB = 1 << 20


def softmax_rows(scores):
    peak = jnp.max(scores, axis=-1, keepdims=True)
    weights = jnp.exp2((scores - peak) * (LOG2E * HD ** -0.5))
    total = jnp.sum(weights, axis=-1, keepdims=True)
    return (weights * (1.0 / total)).astype(jnp.bfloat16)


def local_kernel(per_kv, q_ref, k_ref, v_ref, out_ref):
    start = pl.program_id(1) * BLK
    keys = k_ref[...]
    values = v_ref[...]
    shape = (BLK, keys.shape[0])
    seen = lax.broadcasted_iota(jnp.int32, shape, 1) <= (
        lax.broadcasted_iota(jnp.int32, shape, 0) + start
    )
    for head in range(per_kv):
        cols = slice(head * HD, (head + 1) * HD)
        scores = lax.dot_general(
            q_ref[:, cols], keys, (((1,), (1,)), ((), ())), preferred_element_type=jnp.float32
        )
        weights = softmax_rows(jnp.where(seen, scores, -jnp.inf))
        out_ref[:, cols] = jnp.dot(weights, values, preferred_element_type=jnp.float32)


def local_attention(queries, keys, values, kv_local, per_kv):
    rows = queries.shape[0]
    width = per_kv * HD
    return pl.pallas_call(
        functools.partial(local_kernel, per_kv),
        grid=(kv_local, rows // BLK),
        in_specs=[
            pl.BlockSpec((BLK, width), lambda j, c: (c, j)),
            pl.BlockSpec((rows, HD), lambda j, c: (0, j)),
            pl.BlockSpec((rows, HD), lambda j, c: (0, j)),
        ],
        out_specs=pl.BlockSpec((BLK, width), lambda j, c: (c, j)),
        out_shape=jax.ShapeDtypeStruct(queries.shape, jnp.float32),
        compiler_params=pltpu.CompilerParams(vmem_limit_bytes=40 * MIB),
        cost_estimate=pl.CostEstimate(
            flops=4 * rows * rows * queries.shape[1],
            bytes_accessed=6 * rows * queries.shape[1],
            transcendentals=rows * rows * kv_local * per_kv,
        ),
        name="local_attention",
    )(queries, keys, values)


def weights_kernel(per_kv, topk, slot_ref, q_ref, bias_ref, k_ref, out_ref, picked):
    block = pl.program_id(1)
    for pick in range(topk):
        picked[pick * BLK : (pick + 1) * BLK, :] = k_ref[slot_ref[block * topk + pick]]
    keys = picked[...]
    bias = bias_ref[0]
    for head in range(per_kv):
        scores = lax.dot_general(
            q_ref[:, head * HD : (head + 1) * HD],
            keys,
            (((1,), (1,)), ((), ())),
            preferred_element_type=jnp.float32,
        )
        out_ref[0, 0, head] = softmax_rows(scores + bias)


def memory_weights(slots, queries, bias, keys, kv_local, per_kv, topk):
    rows = queries.shape[0]
    blocks = rows // BLK
    width = topk * BLK
    total = keys.shape[0]
    return pl.pallas_call(
        functools.partial(weights_kernel, per_kv, topk),
        grid_spec=pltpu.PrefetchScalarGridSpec(
            num_scalar_prefetch=1,
            grid=(kv_local, blocks),
            in_specs=[
                pl.BlockSpec((BLK, per_kv * HD), lambda j, c, s: (c, j)),
                pl.BlockSpec((1, 1, width), lambda j, c, s: (c, 0, 0)),
                pl.BlockSpec((total, BLK, HD), lambda j, c, s: (0, 0, j)),
            ],
            out_specs=pl.BlockSpec(
                (1, 1, per_kv, BLK, width), lambda j, c, s: (j, c, 0, 0, 0)
            ),
            scratch_shapes=[pltpu.VMEM((width, HD), jnp.bfloat16)],
        ),
        out_shape=jax.ShapeDtypeStruct((kv_local, blocks, per_kv, BLK, width), jnp.bfloat16),
        compiler_params=pltpu.CompilerParams(vmem_limit_bytes=48 * MIB),
        cost_estimate=pl.CostEstimate(
            flops=2 * rows * width * queries.shape[1],
            bytes_accessed=2 * kv_local * per_kv * rows * width,
            transcendentals=rows * width * kv_local * per_kv,
        ),
        name="memory_weights",
    )(slots, queries, bias, keys)


def mix_kernel(per_kv, topk, first, slot_ref, w_ref, gate_ref, local_ref, v_ref, out_ref, picked):
    block = pl.program_id(1) + first
    for pick in range(topk):
        picked[pick * BLK : (pick + 1) * BLK, :] = v_ref[slot_ref[block * topk + pick]]
    values = picked[...]
    for head in range(per_kv):
        cols = slice(head * HD, (head + 1) * HD)
        mem_out = jnp.dot(w_ref[0, 0, head], values, preferred_element_type=jnp.float32)
        gate = gate_ref[:, cols]
        out_ref[:, cols] = (gate * mem_out + (1.0 - gate) * local_ref[:, cols]).astype(
            jnp.bfloat16
        )


def mix_values(slots, weights, gate, local_out, values, kv_local, per_kv, topk, first, blocks):
    rows, cols = blocks * BLK, local_out.shape[1]
    width = topk * BLK
    total = values.shape[0]
    return pl.pallas_call(
        functools.partial(mix_kernel, per_kv, topk, first),
        grid_spec=pltpu.PrefetchScalarGridSpec(
            num_scalar_prefetch=1,
            grid=(kv_local, blocks),
            in_specs=[
                pl.BlockSpec(
                    (1, 1, per_kv, BLK, width), lambda j, c, s: (j, c + first, 0, 0, 0)
                ),
                pl.BlockSpec((1, per_kv * HD), lambda j, c, s: (0, j)),
                pl.BlockSpec((BLK, per_kv * HD), lambda j, c, s: (c + first, j)),
                pl.BlockSpec((total, BLK, HD), lambda j, c, s: (0, 0, j)),
            ],
            out_specs=pl.BlockSpec((BLK, per_kv * HD), lambda j, c, s: (c, j)),
            scratch_shapes=[pltpu.VMEM((width, HD), jnp.bfloat16)],
        ),
        out_shape=jax.ShapeDtypeStruct((rows, cols), jnp.bfloat16),
        compiler_params=pltpu.CompilerParams(vmem_limit_bytes=48 * MIB),
        cost_estimate=pl.CostEstimate(
            flops=2 * rows * width * cols,
            bytes_accessed=2 * kv_local * per_kv * rows * width,
            transcendentals=0,
        ),
        name="mix_values",
    )(slots, weights, gate, local_out, values)


def plan_requests(flat_chosen, blocks_each):
    owner_of = flat_chosen // blocks_each
    local_of = flat_chosen % blocks_each
    order = jnp.arange(flat_chosen.shape[0])
    repeated = (flat_chosen[:, None] == flat_chosen[None, :]) & (order[None, :] < order[:, None])
    first_seen = jnp.logical_not(jnp.any(repeated, axis=1))
    below = (owner_of[:, None] == owner_of[None, :]) & (flat_chosen[None, :] < flat_chosen[:, None])
    rank_of = jnp.sum((below & first_seen[None, :]).astype(jnp.int32), axis=1)
    return (owner_of, local_of, rank_of, first_seen)


def on_device(
    tokens, w_query, w_key, w_value, w_out, gate_bias, mem_keys, mem_values, block_ids, block_counts
):
    tok_rows = tokens.shape[0]
    qblk_count = tok_rows // BLK
    topk_count = block_ids.shape[1]
    kv_local = w_key.shape[1] // HD
    heads_local = w_query.shape[1] // HD
    per_kv = heads_local // kv_local
    owners = lax.axis_size("mem")
    blocks_each = mem_keys.shape[0] // BLK
    me_index = lax.axis_index("mem")
    capacity = max(2, topk_count * qblk_count // owners)
    all_chosen = lax.all_to_all(
        jnp.broadcast_to(block_ids.reshape(1, -1), (owners, qblk_count * topk_count)),
        "mem",
        split_axis=0,
        concat_axis=0,
        tiled=True,
    )

    def send_list(flat_chosen):
        owner_of, local_of, rank_of, first_seen = plan_requests(flat_chosen, blocks_each)
        wanted = (owner_of == me_index) & first_seen
        select = wanted[None, :] & (rank_of[None, :] == jnp.arange(capacity)[:, None])
        return jnp.sum(select.astype(jnp.int32) * local_of[None, :], axis=1)

    send_slots = jax.vmap(send_list)(all_chosen)
    key_blocks = mem_keys.reshape(blocks_each, BLK, kv_local * HD)
    value_blocks = mem_values.reshape(blocks_each, BLK, kv_local * HD)
    got_keys = lax.all_to_all(
        key_blocks[send_slots], "mem", split_axis=0, concat_axis=0, tiled=True
    ).reshape(owners * capacity, BLK, kv_local * HD)
    got_values = lax.all_to_all(
        value_blocks[send_slots], "mem", split_axis=0, concat_axis=0, tiled=True
    ).reshape(owners * capacity, BLK, kv_local * HD)
    queries = jnp.dot(tokens, w_query, preferred_element_type=jnp.float32).astype(jnp.bfloat16)
    local_keys = jnp.dot(tokens, w_key, preferred_element_type=jnp.float32).astype(jnp.bfloat16)
    local_values = jnp.dot(tokens, w_value, preferred_element_type=jnp.float32).astype(jnp.bfloat16)
    local_out = local_attention(queries, local_keys, local_values, kv_local, per_kv)
    own_flat = block_ids.reshape(-1)
    owner_of, local_of, rank_of, first_seen = plan_requests(own_flat, blocks_each)
    slot_of = owner_of * capacity + rank_of
    total_blocks = block_counts.shape[0]
    filled = jnp.sum(
        jnp.where(own_flat[:, None] == jnp.arange(total_blocks)[None, :], block_counts[None, :], 0),
        axis=1,
    )
    bias = jnp.where(jnp.arange(BLK)[None, :] < filled[:, None], 0.0, -jnp.inf)
    bias = bias.reshape(qblk_count, 1, topk_count * BLK).astype(jnp.float32)
    weights = memory_weights(slot_of, queries, bias, got_keys, kv_local, per_kv, topk_count)
    gate = jnp.repeat(jax.nn.sigmoid(gate_bias), HD).reshape(1, heads_local * HD)
    pieces = []
    half = qblk_count // 2
    for first, count in ((0, half), (half, qblk_count - half)):
        attn = mix_values(
            slot_of, weights, gate, local_out, got_values, kv_local, per_kv, topk_count, first, count
        )
        terms = jnp.dot(attn, w_out, preferred_element_type=jnp.float32).astype(jnp.bfloat16)
        pieces.append(lax.psum_scatter(terms, "head", scatter_dimension=1, tiled=True))
    return jnp.concatenate(pieces, axis=0)


def solution(mesh):
    in_specs = (
        P("mem", None),
        P(None, "head"),
        P(None, "head"),
        P(None, "head"),
        P("head", None),
        P("head"),
        P("mem", "head"),
        P("mem", "head"),
        P("mem", None),
        P(),
    )
    out_specs = P("mem", "head")
    return jax.shard_map(
        on_device, mesh=mesh, in_specs=in_specs, out_specs=out_specs, check_vma=False
    )
```
